32 devices in a mesh: grp: 2 (over y), lon: 4 (over z), lat: 2 (over x), ch: 2 (over core).
Axes of the slice: x: 2, y: 2, z: 4, core: 2. Of those that a mesh axis runs over, the one named last changes fastest.
Arguments:
- fields: bfloat16 [69, 512, 512], P(None, ('grp', 'lat'), 'lon'), parts along dimension 1, may hold values from -6 to 6
- land_sea: int32 [256, 512], P('lat', 'lon'), may hold values 0 or 1
- orography: int32 [256, 512], P('lat', 'lon'), may hold values from 0 to 63
- embed_weight: bfloat16 [69, 4, 4, 512], P(None, None, None, 'ch'), may hold values from -0.1875 to 0.1875
- class_table: bfloat16 [128, 512], P(None, 'ch'), may hold values from -5 to 5
- conv_kernel: float32 [2, 7, 7, 512], P(None, None, None, 'ch'), may hold values from -1.75 to 1.75
- conv_bias: float32 [2, 512], P(None, 'ch'), may hold values from -3 to 3
- norm_gain: float32 [2, 512], replicated, may hold values from 0.5 to 1.5
- norm_bias: float32 [2, 512], replicated, may hold values from -3 to 3
- up_proj: bfloat16 [2, 512, 2048], P(None, 'lon', 'ch'), may hold values from -0.25 to 0.25
- up_bias: float32 [2, 2048], replicated, may hold values from -3 to 3
- down_proj: bfloat16 [2, 2048, 512], P(None, 'ch', 'lon'), may hold values from -0.125 to 0.125
- down_bias: float32 [2, 512], replicated, may hold values from -3 to 3
- layer_scale: float32 [2, 512], replicated, may hold values from 0.25 to 1.75
Outputs:
- features: bfloat16 [128, 128, 512], P(('grp', 'lat'), 'lon', 'ch'), parts along dimension 0
The draws below stay inside these ranges and needn't reach their ends.
There are 2 independent parts, one for each index of `grp`. The reference program is written for one: setup_inputs(seed, part) draws one part's arguments, and reference() takes and returns one part's arrays. A program takes and returns all parts, laid end to end along the dimension named above; an argument that names none is the same for every part. Nothing has to cross between parts.
All inputs are finite; a program needn't handle non-finite values. No bound on the sum of `land_sea` on one device may be relied on, other than what follows from the above.
Results may differ from the reference program's by a relative error of at most 0.014.
Values may be sent and summed in bfloat16 or wider, within the bound.
No kernel may reach another device: no remote copies, remote signals or barrier semaphores. Data moves between devices by JAX's collectives and lax.ppermute only.
A program may use at most 64 MiB of HBM per device.

```python
import jax
import jax.numpy as jnp
from jax import lax

VARS = 69
PATCH = 4
C = 512
HID = 2048
OROG = 64
KERNEL = 7
BLOCKS = 2
HALO = 3
CLASSES = 128
NLAT = 64
NLON = 128
LATC = 256
LONC = 512


def draw_conv_kernel(key, part):
    base = jnp.clip(jax.random.normal(key, (BLOCKS, KERNEL, KERNEL, C), jnp.float32), -4.0, 4.0)
    ramp = 3.0 ** (2.0 * jnp.arange(C, dtype=jnp.float32) / C - 1.0)
    return base * ramp / KERNEL


def set_ends(entries, stream_key, least, high):
    dims = entries.shape
    index_at = [jax.random.randint(jax.random.fold_in(stream_key, axis), (), 0, dims[axis]) for axis in range(len(dims))]
    entries = entries.at[tuple(index_at)].set(least)
    longest = dims.index(max(dims))
    index_at[longest] = (index_at[longest] + 1) % dims[longest]
    return entries.at[tuple(index_at)].set(high)


def block_levels(key, extent, split, least, high):
    loudness = 1.0
    for dim, shards_of in split:
        draws = jax.random.uniform(jax.random.fold_in(jax.random.fold_in(key, 6), dim), (shards_of,), jnp.float32, least / len(split), high / len(split))
        loudness = loudness * jnp.repeat(jnp.exp(draws), extent[dim] // shards_of).reshape((-1,) + (1,) * (len(extent) - 1 - dim))
    return loudness


def gaussian(stream_key, extent, spread, reach, shards=(), kind=jnp.bfloat16):
    array = spread * jax.random.normal(stream_key, extent, jnp.float32)
    if shards:
        array = array * block_levels(stream_key, extent, shards, -0.22, 0.18)
    return jnp.clip(array, -reach, reach).astype(kind)


def setup_inputs(seed: int = 0, part: int = 0) -> dict:
    splits = jax.random.split(jax.random.key(seed), 15)
    own_keys = jax.random.split(jax.random.fold_in(splits[14], part), 15)
    return {
        "fields": gaussian(own_keys[0], (VARS, LATC, LONC), 1.0, 6.0, ((1, 2), (2, 4))),
        "land_sea": set_ends((jax.random.randint(splits[1], (LATC, LONC), 0, 10) < 3).astype(jnp.int32), jax.random.fold_in(splits[1], 1), 0, 1),
        "orography": set_ends(jax.random.randint(splits[2], (LATC, LONC), 0, OROG), jax.random.fold_in(splits[2], 1), 0, OROG - 1).astype(jnp.int32),
        "embed_weight": gaussian(splits[3], (VARS, PATCH, PATCH, C), (VARS * PATCH * PATCH) ** -0.5, 0.1875, ((3, 2),)),
        "class_table": gaussian(splits[4], (CLASSES, C), 1.0, 5.0, ((1, 2),)),
        "conv_kernel": draw_conv_kernel(jax.random.fold_in(splits[14], 71), part),
        "conv_bias": gaussian(splits[6], (BLOCKS, C), 0.5, 3.0, ((1, 2),), jnp.float32),
        "norm_gain": jnp.clip(1.0 + 0.1 * jax.random.normal(splits[7], (BLOCKS, C), jnp.float32), 0.5, 1.5),
        "norm_bias": gaussian(splits[8], (BLOCKS, C), 0.5, 3.0, (), jnp.float32),
        "up_proj": gaussian(splits[9], (BLOCKS, C, HID), C ** -0.5, 0.25, ((1, 4), (2, 2))),
        "up_bias": gaussian(splits[10], (BLOCKS, HID), 0.5, 3.0, (), jnp.float32),
        "down_proj": gaussian(splits[11], (BLOCKS, HID, C), HID ** -0.5, 0.125, ((1, 2), (2, 4))),
        "down_bias": gaussian(splits[12], (BLOCKS, C), 0.5, 3.0, (), jnp.float32),
        "layer_scale": jnp.clip(1.0 + 0.15 * jax.random.normal(splits[13], (BLOCKS, C), jnp.float32), 0.25, 1.75),
    }


def normalize(values, gain, shift):
    average = lax.optimization_barrier(jnp.sum(values, axis=-1, keepdims=True)) / C
    variance = lax.optimization_barrier(jnp.sum(values * values, axis=-1, keepdims=True)) / C - average * average
    return (values - average) * lax.rsqrt(variance + 1e-06) * gain + shift

def reference(fields, land_sea, orography, embed_weight, class_table, conv_kernel, conv_bias, norm_gain, norm_bias, up_proj, up_bias, down_proj, down_bias, layer_scale):
    class_codes = 2 * orography + land_sea
    class_rows = class_table.astype(jnp.float32)
    weight = embed_weight.astype(jnp.float32)
    cell_grid = fields.reshape(VARS, NLAT, PATCH, NLON, PATCH)

    def embed_band(band_row):
        band_block = lax.dynamic_index_in_dim(cell_grid, band_row, 1, keepdims=False).astype(jnp.float32)
        patch_term = jnp.einsum('vpcq,vpqk->ck', band_block, weight)
        code_rows = lax.dynamic_slice_in_dim(class_codes, band_row * PATCH, PATCH, 0)
        one_hot = (code_rows[..., None] == jnp.arange(CLASSES, dtype=jnp.int32)).astype(jnp.float32)
        class_counts = one_hot.reshape(PATCH, NLON, PATCH, CLASSES).sum(axis=(0, 2))
        static_term = jnp.dot(class_counts, class_rows, preferred_element_type=jnp.float32)
        return (patch_term + static_term * (1.0 / (PATCH * PATCH))).astype(jnp.bfloat16)
    stream = lax.map(embed_band, jnp.arange(NLAT, dtype=jnp.int32))
    for layer in range(BLOCKS):
        stream_f = stream.astype(jnp.float32)
        padded = jnp.pad(stream_f, ((HALO, HALO), (0, 0), (0, 0)))
        padded = jnp.concatenate([padded[:, NLON - HALO:], padded, padded[:, :HALO]], axis=1)
        summed = jnp.zeros((NLAT, NLON, C), jnp.float32) + conv_bias[layer]
        for row_off in range(KERNEL):
            for col_off in range(KERNEL):
                summed = summed + padded[row_off:row_off + NLAT, col_off:col_off + NLON] * conv_kernel[layer, row_off, col_off]
        conv = summed.astype(jnp.bfloat16)
        normed = normalize(conv.astype(jnp.float32), norm_gain[layer], norm_bias[layer]).astype(jnp.bfloat16)
        up_weight = up_proj[layer]
        down_weight = down_proj[layer]
        bias_up = up_bias[layer]

        def feed_forward(rows_in):
            pre = jnp.dot(rows_in, up_weight, preferred_element_type=jnp.float32) + bias_up
            hidden = jax.nn.gelu(pre, approximate=True).astype(jnp.bfloat16)
            return jnp.dot(hidden, down_weight, preferred_element_type=jnp.float32)
        update = lax.map(feed_forward, normed)
        stream = (stream_f + layer_scale[layer] * (update + down_bias[layer])).astype(jnp.bfloat16)
    return stream
```

```python
import functools

import jax
import jax.numpy as jnp
from jax import lax
from jax.experimental import pallas as pl
from jax.experimental.pallas import tpu as pltpu
from jax.sharding import PartitionSpec as P

PATCH = 4
KERNEL = 7
BLOCKS = 2
HALO = 3
LANES = 128
VMEM_LIMIT = 60 * 1024 * 1024


def vmem():
    return pl.BlockSpec(memory_space=pltpu.VMEM)


def embed_tokens(fields, land_sea, orography, embed_weight, class_table):
    var_count, lat_cells, lon_cells = fields.shape
    tok_rows = lat_cells // PATCH
    tok_cols = lon_cells // PATCH
    width = embed_weight.shape[3]
    cell_grid = fields.reshape(var_count, tok_rows, PATCH, tok_cols, PATCH)
    patch_term = jnp.einsum(
        "vrpcq,vpqk->rck", cell_grid, embed_weight, preferred_element_type=jnp.float32
    )
    class_codes = 2 * orography + land_sea
    classes = class_table.shape[0]
    one_hot = (class_codes[..., None] == jnp.arange(classes, dtype=jnp.int32)).astype(jnp.bfloat16)
    class_counts = one_hot.reshape(tok_rows, PATCH, tok_cols, PATCH, classes).sum(axis=(1, 3))
    static_term = jnp.dot(
        class_counts.reshape(tok_rows * tok_cols, classes),
        class_table,
        preferred_element_type=jnp.float32,
    )
    return (
        patch_term + static_term.reshape(tok_rows, tok_cols, width) * (1.0 / (PATCH * PATCH))
    ).astype(jnp.bfloat16)


def conv_kernel_body(rows, cols, layer, own, left, right, north, south, kern, bias, gain, shift, out, frame, conv):
    channels = own.shape[2]
    wide = cols + 2 * HALO
    frame[HALO : HALO + rows, HALO : HALO + cols, :] = own[...].astype(jnp.float32)
    frame[HALO : HALO + rows, 0:HALO, :] = left[...].astype(jnp.float32)
    frame[HALO : HALO + rows, HALO + cols : wide, :] = right[...].astype(jnp.float32)
    frame[0:HALO, 0:wide, :] = north[...].astype(jnp.float32)
    frame[HALO + rows : 2 * HALO + rows, 0:wide, :] = south[...].astype(jnp.float32)
    step = 8
    lane_blocks = channels // LANES

    def block(index, carry):
        first = pl.multiple_of((index // lane_blocks) * step, step)
        lanes = pl.ds(pl.multiple_of((index % lane_blocks) * LANES, LANES), LANES)
        sums = [jnp.broadcast_to(bias[layer : layer + 1, lanes], (cols, LANES)) for _ in range(step)]
        for east in range(KERNEL):
            taps = [
                jnp.broadcast_to(kern[layer, down, east : east + 1, lanes], (cols, LANES))
                for down in range(KERNEL)
            ]
            for row in range(step + KERNEL - 1):
                cells = frame[first + row, east : east + cols, lanes]
                for down in range(KERNEL):
                    if 0 <= row - down < step:
                        sums[row - down] = sums[row - down] + cells * taps[down]
        for row in range(step):
            conv[first + row, :, lanes] = sums[row].astype(jnp.bfloat16).astype(jnp.float32)
        return carry

    lax.fori_loop(0, (rows // step) * lane_blocks, block, 0)
    gain_row = gain[layer : layer + 1, :]
    shift_row = shift[layer : layer + 1, :]
    span = 4

    def norm(index, carry):
        first = pl.multiple_of(index * span, span)
        cells = conv[pl.ds(first, span), :, :].reshape(span * cols, channels)
        average = jnp.sum(cells, axis=1, keepdims=True) / channels
        variance = jnp.sum(cells * cells, axis=1, keepdims=True) / channels - average * average
        normed = (cells - average) * lax.rsqrt(variance + 1e-06) * gain_row + shift_row
        out[pl.ds(pl.multiple_of(index * span * cols, span * cols), span * cols), :] = normed.astype(jnp.bfloat16)
        return carry

    lax.fori_loop(0, rows // span, norm, 0)


def conv_norm(layer, own, left, right, north, south, kern, bias, gain, shift):
    rows, cols, channels = own.shape
    return pl.pallas_call(
        functools.partial(conv_kernel_body, rows, cols, layer),
        out_shape=jax.ShapeDtypeStruct((rows * cols, channels), jnp.bfloat16),
        in_specs=[vmem()] * 9,
        out_specs=vmem(),
        scratch_shapes=[
            pltpu.VMEM((rows + 2 * HALO, cols + 8, channels), jnp.float32),
            pltpu.VMEM((rows, cols, channels), jnp.float32),
        ],
        compiler_params=pltpu.CompilerParams(vmem_limit_bytes=VMEM_LIMIT),
        cost_estimate=pl.CostEstimate(flops=100 * rows * cols * channels, bytes_accessed=4 * rows * cols * channels, transcendentals=0),
        name=f"conv_norm_{layer}",
    )(own, left, right, north, south, kern, bias, gain, shift)


def gelu(v):
    return 0.5 * v * (1.0 + jnp.tanh(0.7978845608028654 * (v + 0.044715 * (v * v * v))))


def feed_body(layer, offsets, parts, halves, x, stream, bias_up, bias_down, scale, *refs):
    pieces = [refs[h * parts : (h + 1) * parts] for h in range(halves)]
    out, x_scr, total = refs[halves * parts :]
    tokens, channels = x.shape
    width = channels // parts
    half = bias_up.shape[1] // halves
    spots, up_at, down_at, core = offsets()
    for k in range(parts):
        x_scr[:, width * k : width * (k + 1)] = x[:, pl.ds(pl.multiple_of(spots[k] * width, width), width)]
    total[...] = jnp.zeros_like(total)
    chunk = 2 * LANES

    def step(j, carry):
        for h in range(halves):
            mine = pieces[h]
            ups, downs = [], []
            for k in range(parts):
                lo = pl.multiple_of(j * 2 * width, 2 * width)
                both = mine[k][up_at[k], pl.ds(lo, 2 * width), :]
                ups.append(jnp.concatenate([both[:width], both[width:]], axis=1))
                downs.append(mine[k][down_at[k], pl.ds(pl.multiple_of(j * chunk, chunk), chunk), :])
            up_w = jnp.concatenate(ups, axis=0)
            down_w = jnp.concatenate(downs, axis=1)
            owner = core if h == 0 else 1 - core
            bias = bias_up[layer : layer + 1, pl.ds(pl.multiple_of(owner * half + j * chunk, chunk), chunk)]
            pre = jnp.dot(x_scr[...], up_w, preferred_element_type=jnp.float32) + bias
            hidden = gelu(pre).astype(jnp.bfloat16)
            total[...] += jnp.dot(hidden, down_w, preferred_element_type=jnp.float32)
        return carry

    lax.fori_loop(0, half // chunk, step, 0)
    for k in range(parts):
        lanes = pl.ds(pl.multiple_of(spots[k] * width, width), width)
        update = total[:, width * k : width * (k + 1)]
        out[:, lanes] = (
            stream[:, lanes].astype(jnp.float32)
            + scale[layer : layer + 1, lanes] * (update + bias_down[layer : layer + 1, lanes])
        ).astype(jnp.bfloat16)


def feed_pieces(layer, x, stream, bias_up, bias_down, scale, mine, theirs):
    tokens, channels = x.shape
    parts = len(mine)

    def offsets():
        z, lat, grp, core = (lax.axis_index(a) for a in ("lon", "lat", "grp", "ch"))
        z1 = z + 1 - 2 * lax.rem(z, 2)
        far = lax.rem(z + 2, 4)
        far1 = lax.rem(z1 + 2, 4)
        p = far + lat * (far1 - far)
        q = far1 + lat * (far - far1)
        return [z, z1, p, q], [0, 0, grp, grp], [1, 1, 1 - grp, 1 - grp], core

    tokens_hidden = tokens * bias_up.shape[1]
    return pl.pallas_call(
        functools.partial(feed_body, layer, offsets, parts, 2),
        out_shape=jax.ShapeDtypeStruct((tokens, channels), jnp.bfloat16),
        in_specs=[vmem()] * (5 + 2 * parts),
        out_specs=vmem(),
        scratch_shapes=[
            pltpu.VMEM((tokens, channels), jnp.bfloat16),
            pltpu.VMEM((tokens, channels), jnp.float32),
        ],
        compiler_params=pltpu.CompilerParams(vmem_limit_bytes=VMEM_LIMIT),
        cost_estimate=pl.CostEstimate(flops=4 * tokens_hidden * channels, bytes_accessed=6 * 2**20, transcendentals=tokens_hidden),
        name=f"feed_{layer}",
    )(x, stream, bias_up, bias_down, scale, *mine, *theirs)


def feed_plain(layer, x, stream, bias_up, bias_down, scale, up, down):
    pre = jnp.dot(x, up, preferred_element_type=jnp.float32) + bias_up[layer]
    hidden = jax.nn.gelu(pre, approximate=True).astype(jnp.bfloat16)
    update = jnp.dot(hidden, down, preferred_element_type=jnp.float32)
    return (stream.astype(jnp.float32) + scale[layer] * (update + bias_down[layer])).astype(jnp.bfloat16)


def pack_body(up, down, *outs):
    blocks = up.shape[2] // LANES
    depth = up.shape[1]
    for layer, out in enumerate(outs):
        for b in range(blocks):
            out[0, b * depth : (b + 1) * depth, :] = up[layer, :, b * LANES : (b + 1) * LANES]
        out[1, :, :] = down[layer]


def pack_weights(up, down):
    blocks, depth, half, width = up.shape[0], up.shape[1], down.shape[1], down.shape[2]
    return pl.pallas_call(
        pack_body,
        out_shape=[jax.ShapeDtypeStruct((2, half, width), jnp.bfloat16)] * blocks,
        in_specs=[vmem()] * 2,
        out_specs=[vmem()] * blocks,
        compiler_params=pltpu.CompilerParams(vmem_limit_bytes=VMEM_LIMIT),
        name="pack",
    )(up, down)


def swap(value, axis):
    return lax.ppermute(value, axis, [(0, 1), (1, 0)])


def spread_pieces(packed):
    z_count, lat_count = lax.axis_size("lon"), lax.axis_size("lat")
    grp = lax.axis_index("grp")
    cross = []
    for z in range(z_count):
        for lat in range(lat_count):
            cross.append((z * lat_count + lat, (z ^ (2 + lat)) * lat_count + lat))
    part = lax.dynamic_index_in_dim(packed, grp, 0, keepdims=True)
    far = lax.ppermute(part, ("lon", "lat"), cross)
    near = lax.ppermute(packed, "lon", [(z, z ^ 1) for z in range(z_count)])
    other = swap(far, "grp")
    held = jnp.concatenate([far, other], axis=0)
    last = swap(held, "lat")
    mine = [packed, near, held, last]
    return mine, [swap(piece, "ch") for piece in mine]


def exchange(edge_low, edge_high, axis, closed):
    count = lax.axis_size(axis)
    ends = count if closed else count - 1
    if count == 2 and not closed:
        index = lax.axis_index(axis)
        got = swap(jnp.where(index == 0, edge_high, edge_low), axis)
        zero = jnp.zeros_like(got)
        return jnp.where(index == 0, zero, got), jnp.where(index == 0, got, zero)
    return (
        lax.ppermute(edge_high, axis, [(i, (i + 1) % count) for i in range(ends)]),
        lax.ppermute(edge_low, axis, [((i + 1) % count, i) for i in range(ends)]),
    )


def halos(stream):
    rows, cols, channels = stream.shape
    core = lax.axis_index("ch")
    z_count = lax.axis_size("lon")
    west_edge, east_edge = stream[:, :HALO], stream[:, cols - HALO :]
    outward = jnp.where(core == 0, west_edge, east_edge)
    inward = jnp.where(core == 0, east_edge, west_edge)
    pairs = []
    for z in range(z_count):
        up = (z + 1) % z_count
        pairs += [(2 * z + 1, 2 * up), (2 * up, 2 * z + 1)]
    outer = lax.ppermute(outward, ("lon", "ch"), pairs)
    inner = swap(inward, "ch")
    west = jnp.where(core == 0, outer, inner)
    east = jnp.where(core == 0, inner, outer)
    low = jnp.concatenate([west[:HALO], stream[:HALO], east[:HALO]], axis=1)
    high = jnp.concatenate([west[rows - HALO :], stream[rows - HALO :], east[rows - HALO :]], axis=1)
    north, south = exchange(low, high, "lat", False)
    return west, east, north, south


def body(
    fields,
    land_sea,
    orography,
    embed_weight,
    class_table,
    conv_kernel,
    conv_bias,
    norm_gain,
    norm_bias,
    up_proj,
    up_bias,
    down_proj,
    down_bias,
    layer_scale,
):
    core = lax.axis_index("ch")
    cores = lax.axis_size("ch")
    fast = (
        lax.axis_size("lon") == 4
        and lax.axis_size("lat") == 2
        and lax.axis_size("grp") == 2
        and down_proj.shape[2] == LANES
    )
    if fast:
        packed = pack_weights(up_proj, down_proj)
        weights = [spread_pieces(piece) for piece in packed]
    else:
        up_full = lax.all_gather(lax.all_gather(up_proj, "ch", axis=2, tiled=True), "lon", axis=1, tiled=True)
        down_full = lax.all_gather(lax.all_gather(down_proj, "ch", axis=1, tiled=True), "lon", axis=2, tiled=True)
        weights = [(up_full[layer], down_full[layer]) for layer in range(BLOCKS)]
    feed = feed_pieces if fast else feed_plain

    gather = functools.partial(lax.all_gather, axis_name="ch", tiled=True)
    embed_full = gather(embed_weight, axis=3)
    table_full = gather(class_table, axis=1)
    kern_full = gather(conv_kernel, axis=3)
    bias_full = gather(conv_bias, axis=1)
    tokens = embed_tokens(fields, land_sea, orography, embed_full, table_full)
    rows, all_cols, channels = tokens.shape
    cols = all_cols // cores
    stream = lax.dynamic_slice_in_dim(tokens, core * cols, cols, axis=1)
    for layer in range(BLOCKS):
        west, east, north, south = halos(stream)
        normed = conv_norm(layer, stream, west, east, north, south, kern_full, bias_full, norm_gain, norm_bias)
        flat = feed(layer, normed, stream.reshape(rows * cols, channels), up_bias, down_bias, layer_scale, *weights[layer])
        stream = flat.reshape(rows, cols, channels)
    share = channels // cores
    keep = lax.dynamic_slice_in_dim(stream, core * share, share, axis=2)
    give = lax.dynamic_slice_in_dim(stream, (1 - core) * share, share, axis=2)
    got = swap(give, "ch")
    first = jnp.where(core == 0, keep, got)
    second = jnp.where(core == 0, got, keep)
    return jnp.concatenate([first, second], axis=1)


def solution(mesh):
    in_specs = (
        P(None, ("grp", "lat"), "lon"),
        P("lat", "lon"),
        P("lat", "lon"),
        P(None, None, None, "ch"),
        P(None, "ch"),
        P(None, None, None, "ch"),
        P(None, "ch"),
        P(),
        P(),
        P(None, "lon", "ch"),
        P(),
        P(None, "ch", "lon"),
        P(),
        P(),
    )
    out_specs = P(("grp", "lat"), "lon", "ch")
    return jax.shard_map(body, mesh=mesh, in_specs=in_specs, out_specs=out_specs, check_vma=False)
```

```python
import functools

import jax
import jax.numpy as jnp
from jax import lax
from jax.experimental import pallas as pl
from jax.experimental.pallas import tpu as pltpu
from jax.sharding import PartitionSpec as P

PATCH = 4
KERNEL = 7
BLOCKS = 2
HALO = 3
LANES = 128
VMEM_LIMIT = 20 * 2**20


def vmem():
    return pl.BlockSpec(memory_space=pltpu.VMEM)


def after(value, *others):
    return lax.optimization_barrier((value, *others))[0]


def edge_shapes(rows, cols, channels):
    kinds = 1 if lax.axis_size("lat") == 2 else 2
    shapes = [(rows, HALO, channels)] * 2
    for _ in range(kinds):
        shapes += [(HALO, cols, channels), (HALO, HALO, channels), (HALO, HALO, channels)]
    return [jax.ShapeDtypeStruct(shape, jnp.bfloat16) for shape in shapes]


def emit_edges(tokens, outs):
    rows, cols = tokens.shape[0], tokens.shape[1]
    west_core = lax.axis_index("ch") == 0
    west, east = tokens[:, :HALO].astype(jnp.float32), tokens[:, cols - HALO :].astype(jnp.float32)
    outward, inward = jnp.where(west_core, west, east), jnp.where(west_core, east, west)
    outs[0][...] = outward.astype(jnp.bfloat16)
    outs[1][...] = inward.astype(jnp.bfloat16)
    first, last = slice(0, HALO), slice(rows - HALO, rows)
    sources = [tokens.astype(jnp.float32), outward, inward]
    for k, source in enumerate(sources):
        if len(outs) == 5:
            outs[2 + k][...] = jnp.where(lax.axis_index("lat") == 0, source[last], source[first]).astype(jnp.bfloat16)
        else:
            outs[2 + k][...] = source[first].astype(jnp.bfloat16)
            outs[5 + k][...] = source[last].astype(jnp.bfloat16)


def send_edges(edges):
    z_count, lat_count = lax.axis_size("lon"), lax.axis_size("lat")
    partner = {}
    for z in range(z_count):
        partner[z, 1] = ((z + 1) % z_count, 0)
        partner[(z + 1) % z_count, 0] = (z, 1)
    spots = [(z, c) for z in range(z_count) for c in range(2)]
    outer = lax.ppermute(edges[0], ("lon", "ch"), [(2 * z + c, 2 * partner[z, c][0] + partner[z, c][1]) for z, c in spots])
    inner = swap(edges[1], "ch")

    def along(group, moves):
        far = []
        for a, b in moves:
            for z, c in spots:
                y, d = partner[z, c]
                far.append(((z * lat_count + a) * 2 + c, (y * lat_count + b) * 2 + d))
        near = [(2 * a + c, 2 * b + 1 - c) for a, b in moves for c in range(2)]
        return [
            lax.ppermute(group[0], "lat", moves),
            lax.ppermute(group[1], ("lon", "lat", "ch"), far),
            lax.ppermute(group[2], ("lat", "ch"), near),
        ]

    if lat_count == 2:
        got = along(edges[2:], [(0, 1), (1, 0)])
        return [outer, inner, *got, *got]
    south = along(edges[2:5], [(i + 1, i) for i in range(lat_count - 1)])
    north = along(edges[5:8], [(i, i + 1) for i in range(lat_count - 1)])
    return [outer, inner, *north, *south]


def swap(value, axis):
    return lax.ppermute(value, axis, [(0, 1), (1, 0)])


def embed_body(cols, pad, fields, land_sea, orography, weight, weight2, table, table2, out, *refs):
    edges, (select, gathered) = refs[:-2], refs[-2:]
    var_count, lat_cells, lon_cells = fields.shape
    tok_rows = lat_cells // PATCH
    taps = PATCH * PATCH
    classes = table.shape[0]
    groups = LANES // cols
    per = tok_rows // groups
    chunk = per * PATCH
    wide = PATCH * LANES
    core = lax.axis_index("ch")
    col = lax.broadcasted_iota(jnp.int32, (8, wide), 1)
    cell = PATCH * (core * cols + col % cols) + col // LANES
    target = (col % LANES) // cols * lon_cells + cell
    line = lax.broadcasted_iota(jnp.int32, (8, wide), 0)
    for row in range(0, groups * lon_cells, 16):
        lower = jnp.where(line + row == target, 1.0, 0.0)
        upper = jnp.where(line + (row + 8) == target, 1.0, 0.0)
        select[row : row + 16, :] = jnp.concatenate([lower, upper], axis=0).astype(jnp.bfloat16)
    spare = pad * chunk - (var_count + 1) * chunk
    gathered[:, (var_count + 1) * chunk :, :] = jnp.zeros((PATCH, spare, LANES), jnp.float32)

    def keep(first, count, rows):
        for q in range(PATCH):
            gathered[q, pl.ds(first, count), :] = rows[:, q * LANES : (q + 1) * LANES]

    codes = (2 * orography[...] + land_sea[...]).astype(jnp.float32).astype(jnp.bfloat16)
    lines = jnp.concatenate([codes[g * chunk : (g + 1) * chunk, :] for g in range(groups)], axis=1)
    keep(var_count * chunk, chunk, jnp.dot(lines, select[...], preferred_element_type=jnp.float32))
    batch = next(n for n in (23, 8, 4, 2, 1) if var_count % n == 0)

    def regroup(index, carry):
        first = index * batch
        parts = [
            fields[pl.ds(first, batch), g * chunk : (g + 1) * chunk, :].reshape(batch * chunk, lon_cells)
            for g in range(groups)
        ]
        rows = jnp.dot(jnp.concatenate(parts, axis=1), select[...], preferred_element_type=jnp.float32)
        keep(pl.multiple_of(first * chunk, chunk), batch * chunk, rows)
        return carry

    lax.fori_loop(0, var_count // batch, regroup, 0)
    kinds = lax.broadcasted_iota(jnp.int32, (classes, LANES), 0).astype(jnp.float32)
    sides = []
    for sub in range(per):
        stack = []
        count = jnp.zeros((classes, LANES), jnp.float32)
        for tap in range(taps):
            p, q = tap // PATCH, tap % PATCH
            stack.append(gathered[q, pl.ds(sub * PATCH + p, pad, stride=chunk), :].astype(jnp.bfloat16))
            spot = var_count * chunk + sub * PATCH + p
            count = count + jnp.where(gathered[q, spot : spot + 1, :] == kinds, 1.0 / taps, 0.0)
        stack.append(count.astype(jnp.bfloat16))
        sides.append(jnp.concatenate(stack, axis=0))
    left = jnp.concatenate(sides, axis=1)
    share = weight.shape[1]
    for side, owner in ((weight, table), core), ((weight2, table2), 1 - core):
        right = jnp.concatenate([ref[...] for ref in side], axis=0)
        tokens = lax.dot_general(left, right, (((0,), (0,)), ((), ())), preferred_element_type=jnp.float32)
        tokens = tokens.astype(jnp.bfloat16)
        lanes = pl.ds(pl.multiple_of(owner * share, share), share)
        for sub in range(per):
            for g in range(groups):
                at = sub * LANES + g * cols
                out[g * per + sub, :, lanes] = tokens[at : at + cols, :]
    emit_edges(out[...], edges)


def embed_tokens(fields, land_sea, orography, weight, weight2, table, table2, cols):
    var_count, lat_cells, lon_cells = fields.shape
    tok_rows = lat_cells // PATCH
    pad = weight.shape[0] // (PATCH * PATCH)
    channels = 2 * weight.shape[1]
    groups = LANES // cols
    edges = edge_shapes(tok_rows, cols, channels)
    return pl.pallas_call(
        functools.partial(embed_body, cols, pad),
        out_shape=[jax.ShapeDtypeStruct((tok_rows, cols, channels), jnp.bfloat16), *edges],
        in_specs=[vmem()] * 7,
        out_specs=[vmem()] * (1 + len(edges)),
        scratch_shapes=[
            pltpu.VMEM((groups * lon_cells, PATCH * LANES), jnp.bfloat16),
            pltpu.VMEM((PATCH, pad * lat_cells // groups, LANES), jnp.float32),
        ],
        compiler_params=pltpu.CompilerParams(vmem_limit_bytes=24 * 2**20),
        cost_estimate=pl.CostEstimate(flops=3 * 10**9, bytes_accessed=5 * 10**6, transcendentals=0),
        name="embed",
    )(fields, land_sea, orography, weight, weight2, table, table2)


def tap_weights(embed_weight):
    var_count, width = embed_weight.shape[0], embed_weight.shape[3]
    pad = (var_count + 1 + 15) // 16 * 16
    turned = embed_weight.reshape(var_count, PATCH * PATCH, width).transpose(1, 0, 2)
    turned = jnp.pad(turned, ((0, 0), (0, pad - var_count), (0, 0)))
    return turned.reshape(PATCH * PATCH * pad, width)


def conv_kernel_body(rows, cols, layer, lat_count, own, *refs):
    outer, inner, north, north_out, north_in, south, south_out, south_in = refs[:8]
    kern_own, kern_other, gain, shift, out, frame, conv, kern = refs[8:]
    channels = own.shape[2]
    share = kern_own.shape[2]
    core, lat = lax.axis_index("ch"), lax.axis_index("lat")
    wide = cols + 2 * HALO
    step = 8
    lane_blocks = channels // LANES
    kern[:, pl.ds(pl.multiple_of(core * share, share), share)] = kern_own[layer]
    kern[:, pl.ds(pl.multiple_of((1 - core) * share, share), share)] = kern_other[layer]
    upper, middle, lower = slice(0, HALO), slice(HALO, HALO + rows), slice(HALO + rows, 2 * HALO + rows)
    centre, bands = slice(HALO, HALO + cols), (slice(0, HALO), slice(HALO + cols, wide))

    def fill(spot, columns, ref, live=None):
        for b in range(lane_blocks):
            cells = ref[:, :, b * LANES : (b + 1) * LANES].astype(jnp.float32)
            if live is not None:
                cells = jnp.where(live, cells, 0.0)
            frame[b, spot, columns, :] = cells

    fill(middle, centre, own)
    fill(upper, centre, north, lat > 0)
    fill(lower, centre, south, lat < lat_count - 1)
    for west_core in range(2):

        @pl.when(core == west_core)
        def _():
            outside, inside = bands[west_core], bands[1 - west_core]
            fill(middle, outside, outer)
            fill(middle, inside, inner)
            fill(upper, outside, north_out, lat > 0)
            fill(upper, inside, north_in, lat > 0)
            fill(lower, outside, south_out, lat < lat_count - 1)
            fill(lower, inside, south_in, lat < lat_count - 1)

    def block(index, carry):
        first = pl.multiple_of((index // lane_blocks) * step, step)
        lanes = pl.ds(pl.multiple_of((index % lane_blocks) * LANES, LANES), LANES)
        sums = [jnp.broadcast_to(kern[KERNEL * KERNEL : KERNEL * KERNEL + 1, lanes], (cols, LANES)) for _ in range(step)]
        for east in range(KERNEL):
            taps = [
                jnp.broadcast_to(kern[KERNEL * down + east : KERNEL * down + east + 1, lanes], (cols, LANES))
                for down in range(KERNEL)
            ]
            for row in range(step + KERNEL - 1):
                cells = frame[index % lane_blocks, first + row, east : east + cols, :]
                for down in range(KERNEL):
                    if 0 <= row - down < step:
                        sums[row - down] = sums[row - down] + cells * taps[down]
        for row in range(step):
            conv[first + row, :, lanes] = sums[row].astype(jnp.bfloat16).astype(jnp.float32)
        return carry

    lax.fori_loop(0, (rows // step) * lane_blocks, block, 0)
    gain_row = gain[layer : layer + 1, :]
    shift_row = shift[layer : layer + 1, :]
    span = 4

    def norm(index, carry):
        first = pl.multiple_of(index * span, span)
        cells = conv[pl.ds(first, span), :, :].reshape(span * cols, channels)
        average = jnp.sum(cells, axis=1, keepdims=True) / channels
        variance = jnp.sum(cells * cells, axis=1, keepdims=True) / channels - average * average
        normed = (cells - average) * lax.rsqrt(variance + 1e-06) * gain_row + shift_row
        out[pl.ds(pl.multiple_of(index * span * cols, span * cols), span * cols), :] = normed.astype(jnp.bfloat16)
        return carry

    lax.fori_loop(0, rows // span, norm, 0)


def conv_norm(layer, own, halo, kern_own, kern_other, gain, shift):
    rows, cols, channels = own.shape
    return pl.pallas_call(
        functools.partial(conv_kernel_body, rows, cols, layer, lax.axis_size("lat")),
        out_shape=jax.ShapeDtypeStruct((rows * cols, channels), jnp.bfloat16),
        in_specs=[vmem()] * (5 + len(halo)),
        out_specs=vmem(),
        scratch_shapes=[
            pltpu.VMEM((channels // LANES, rows + 2 * HALO, cols + 8, LANES), jnp.float32),
            pltpu.VMEM((rows, cols, channels), jnp.float32),
            pltpu.VMEM((kern_own.shape[1], channels), jnp.float32),
        ],
        compiler_params=pltpu.CompilerParams(vmem_limit_bytes=VMEM_LIMIT),
        cost_estimate=pl.CostEstimate(flops=100 * rows * cols * channels, bytes_accessed=4 * rows * cols * channels, transcendentals=0),
        name=f"conv_norm_{layer}",
    )(own, *halo, kern_own, kern_other, gain, shift)


def gelu(v):
    half = 0.5 * v
    return half + half * jnp.tanh(v * (0.7978845608028654 + 0.7978845608028654 * 0.044715 * (v * v)))


def places():
    z, lat, grp = (lax.axis_index(a) for a in ("lon", "lat", "grp"))
    z1 = z + 1 - 2 * lax.rem(z, 2)
    far, far1 = lax.rem(z + 2, 4), lax.rem(z1 + 2, 4)
    return [z, z1, far + lat * (far1 - far), far1 + lat * (far - far1)], [0, 0, grp, grp]


def feed_body(layer, parts, final, x, stream, bias_up, bias_down, scale, *refs):
    pieces = refs[: 2 * parts]
    outs, (whole, x_scr, total) = refs[2 * parts : -3], refs[-3:]
    tokens, channels = x.shape
    width = channels // parts
    half = bias_up.shape[1] // 2
    chunk = 2 * width
    spots, up_at = places()
    core = lax.axis_index("ch")
    j = pl.program_id(0)

    @pl.when(j == 0)
    def _():
        for k in range(parts):
            x_scr[:, width * k : width * (k + 1)] = x[:, pl.ds(pl.multiple_of(spots[k] * width, width), width)]

    ups, downs, biases = [], [], []
    for h, owner in enumerate((core, 1 - core)):
        mine = pieces[h * parts : (h + 1) * parts]
        both = [ref[at] for ref, at in zip(mine, up_at)]
        ups.append(jnp.concatenate([jnp.concatenate([b[:width], b[width:]], axis=1) for b in both], axis=0))
        downs.append(jnp.concatenate([ref[1 - at] for ref, at in zip(mine, up_at)], axis=1))
        biases.append(bias_up[layer : layer + 1, pl.ds(pl.multiple_of(owner * half + j * chunk, chunk), chunk)])
    pre = jnp.dot(x_scr[...], jnp.concatenate(ups, axis=1), preferred_element_type=jnp.float32)
    hidden = gelu(pre + jnp.concatenate(biases, axis=1)).astype(jnp.bfloat16)
    update = jnp.dot(hidden, jnp.concatenate(downs, axis=0), preferred_element_type=jnp.float32)

    @pl.when(j == 0)
    def _():
        total[...] = update

    @pl.when(j > 0)
    def _():
        total[...] += update

    @pl.when(j == pl.num_programs(0) - 1)
    def _():
        for k in range(parts):
            lanes = pl.ds(pl.multiple_of(spots[k] * width, width), width)
            change = total[:, width * k : width * (k + 1)]
            whole[:, lanes] = (
                stream[:, lanes].astype(jnp.float32)
                + scale[layer : layer + 1, lanes] * (change + bias_down[layer : layer + 1, lanes])
            ).astype(jnp.bfloat16)
        if final:
            share = channels // 2
            for ref, owner in zip(outs, (core, 1 - core)):
                ref[...] = whole[:, pl.ds(pl.multiple_of(owner * share, share), share)].reshape(ref.shape)
        else:
            outs[0][...] = whole[...].reshape(outs[0].shape)
            emit_edges(outs[0][...], outs[1:])


def feed_pieces(layer, x, stream, bias_up, bias_down, scale, mine, theirs):
    rows, cols, channels = stream.shape
    tokens = rows * cols
    parts = len(mine)
    final = layer == BLOCKS - 1
    if final:
        shapes = [jax.ShapeDtypeStruct((rows, cols, channels // 2), jnp.bfloat16)] * 2
    else:
        shapes = [jax.ShapeDtypeStruct((rows, cols, channels), jnp.bfloat16), *edge_shapes(rows, cols, channels)]
    steps = mine[0].shape[1] // (2 * LANES)
    piece = pl.BlockSpec((2, 2 * LANES, LANES), lambda j: (0, j, 0))
    tokens_hidden = tokens * bias_up.shape[1]
    return pl.pallas_call(
        functools.partial(feed_body, layer, parts, final),
        grid=(steps,),
        out_shape=shapes,
        in_specs=[vmem()] * 5 + [piece] * (2 * parts),
        out_specs=[vmem()] * len(shapes),
        scratch_shapes=[
            pltpu.VMEM((tokens, channels), jnp.bfloat16),
            pltpu.VMEM((tokens, channels), jnp.bfloat16),
            pltpu.VMEM((tokens, channels), jnp.float32),
        ],
        compiler_params=pltpu.CompilerParams(vmem_limit_bytes=VMEM_LIMIT),
        cost_estimate=pl.CostEstimate(flops=4 * tokens_hidden * channels, bytes_accessed=6 * 2**20, transcendentals=tokens_hidden),
        name=f"feed_{layer}",
    )(x, stream.reshape(tokens, channels), bias_up, bias_down, scale, *mine, *theirs)


def feed_plain(layer, x, stream, bias_up, bias_down, scale, up, down):
    rows, cols, channels = stream.shape
    pre = jnp.dot(x, up, preferred_element_type=jnp.float32) + bias_up[layer]
    hidden = jax.nn.gelu(pre, approximate=True).astype(jnp.bfloat16)
    update = jnp.dot(hidden, down, preferred_element_type=jnp.float32).reshape(rows, cols, channels)
    stream = (stream.astype(jnp.float32) + scale[layer] * (update + bias_down[layer])).astype(jnp.bfloat16)
    if layer == BLOCKS - 1:
        share = channels // 2
        core = lax.axis_index("ch")
        return [lax.dynamic_slice_in_dim(stream, owner * share, share, axis=2) for owner in (core, 1 - core)]
    edges = edge_shapes(rows, cols, channels)
    return pl.pallas_call(
        lambda tokens, *outs: emit_edges_of(tokens, outs),
        out_shape=[jax.ShapeDtypeStruct(stream.shape, jnp.bfloat16), *edges],
        in_specs=[vmem()],
        out_specs=[vmem()] * (1 + len(edges)),
        compiler_params=pltpu.CompilerParams(vmem_limit_bytes=VMEM_LIMIT),
        name="edges",
    )(stream)


def emit_edges_of(tokens, outs):
    outs[0][...] = tokens[...]
    emit_edges(tokens[...], outs[1:])


def pack_body(up, down, packed, part):
    depth = up.shape[1]
    for b in range(up.shape[2] // LANES):
        packed[0, b * depth : (b + 1) * depth, :] = up[0, :, b * LANES : (b + 1) * LANES]
    packed[1, :, :] = down[0]
    part[...] = packed[pl.ds(lax.axis_index("grp"), 1)]


def pack_weights(layer, up, down):
    half, width = down.shape[1], down.shape[2]
    return pl.pallas_call(
        pack_body,
        grid=(1,),
        out_shape=[
            jax.ShapeDtypeStruct((2, half, width), jnp.bfloat16),
            jax.ShapeDtypeStruct((1, half, width), jnp.bfloat16),
        ],
        in_specs=[
            pl.BlockSpec((1, *up.shape[1:]), lambda i: (layer, 0, 0)),
            pl.BlockSpec((1, *down.shape[1:]), lambda i: (layer, 0, 0)),
        ],
        out_specs=[vmem()] * 2,
        compiler_params=pltpu.CompilerParams(vmem_limit_bytes=VMEM_LIMIT),
        name=f"pack_{layer}",
    )(up, down)


def join_body(first, second, out):
    out[0] = first[0]
    out[1] = second[0]


def join(first, second):
    return pl.pallas_call(
        join_body,
        out_shape=jax.ShapeDtypeStruct((2, *first.shape[1:]), first.dtype),
        in_specs=[vmem()] * 2,
        out_specs=vmem(),
        compiler_params=pltpu.CompilerParams(vmem_limit_bytes=VMEM_LIMIT),
        name="join",
    )(first, second)


def fetch_far(part):
    z_count, lat_count = lax.axis_size("lon"), lax.axis_size("lat")
    cross = [(z * lat_count + lat, (z ^ (2 + lat)) * lat_count + lat) for z in range(z_count) for lat in range(lat_count)]
    return lax.ppermute(part, ("lon", "lat"), cross)


def fetch_near(packed):
    return lax.ppermute(packed, "lon", [(z, z ^ 1) for z in range(lax.axis_size("lon"))])


def merge_body(keep, got, out):
    cols = keep.shape[1]
    core = lax.axis_index("ch")
    out[:, pl.ds(pl.multiple_of(core * cols, cols), cols), :] = keep[...]
    out[:, pl.ds(pl.multiple_of((1 - core) * cols, cols), cols), :] = got[...]


def merge(keep, got):
    rows, cols, share = keep.shape
    return pl.pallas_call(
        merge_body,
        out_shape=jax.ShapeDtypeStruct((rows, 2 * cols, share), jnp.bfloat16),
        in_specs=[vmem()] * 2,
        out_specs=vmem(),
        compiler_params=pltpu.CompilerParams(vmem_limit_bytes=VMEM_LIMIT),
        name="merge",
    )(keep, got)


def body(
    fields,
    land_sea,
    orography,
    embed_weight,
    class_table,
    conv_kernel,
    conv_bias,
    norm_gain,
    norm_bias,
    up_proj,
    up_bias,
    down_proj,
    down_bias,
    layer_scale,
):
    cores = lax.axis_size("ch")
    fast = (
        lax.axis_size("lon") == 4
        and lax.axis_size("lat") == 2
        and lax.axis_size("grp") == 2
        and down_proj.shape[2] == LANES
    )
    cols = fields.shape[2] // PATCH // cores
    blocks, _, _, share = conv_kernel.shape
    taps = jnp.concatenate([conv_kernel.reshape(blocks, KERNEL * KERNEL, share), conv_bias[:, None]], axis=1)
    weight = tap_weights(embed_weight)

    if fast:
        packed0, part0 = pack_weights(0, up_proj, down_proj)
        far0 = fetch_far(part0)
        weight = after(weight, part0)
    weight2, table2, taps2 = swap(weight, "ch"), swap(class_table, "ch"), swap(taps, "ch")
    stream, *edges = embed_tokens(fields, land_sea, orography, weight, weight2, class_table, table2, cols)
    halo = send_edges(edges)
    conv = functools.partial(conv_norm, kern_own=taps, kern_other=taps2, gain=norm_gain, shift=norm_bias)
    if not fast:
        up_full = lax.all_gather(lax.all_gather(up_proj, "ch", axis=2, tiled=True), "lon", axis=1, tiled=True)
        down_full = lax.all_gather(lax.all_gather(down_proj, "ch", axis=1, tiled=True), "lon", axis=2, tiled=True)
        for layer in range(BLOCKS):
            normed = conv(layer, stream, halo)
            stream, *edges = feed_plain(
                layer, normed, stream, up_bias, down_bias, layer_scale, up_full[layer], down_full[layer]
            )
            if layer < BLOCKS - 1:
                halo = send_edges(edges)
        return merge(stream, swap(edges[0], "ch"))

    packed0 = after(packed0, stream)
    near0 = fetch_near(packed0)
    far0 = after(far0, stream)
    held0 = join(far0, swap(far0, "grp"))
    last0 = swap(held0, "lat")
    up1, down1 = after((up_proj, down_proj), stream)
    packed1, part1 = pack_weights(1, up1, down1)
    far1 = fetch_far(after(part1, held0))
    mine0 = [packed0, near0, held0, last0]
    theirs0 = [swap(piece, "ch") for piece in mine0]
    normed = conv(0, after(stream, held0), halo)
    far1 = after(far1, normed)
    other1 = swap(far1, "grp")
    near1 = fetch_near(after(packed1, normed))
    stream, *edges = feed_pieces(0, normed, stream, up_bias, down_bias, layer_scale, mine0, theirs0)
    halo = send_edges(edges)
    held1 = join(far1, after(other1, stream))
    last1 = swap(held1, "lat")
    mine1 = [packed1, near1, held1, last1]
    theirs1 = [swap(piece, "ch") for piece in mine1]
    normed = conv(1, stream, halo)
    keep, give = feed_pieces(1, normed, stream, up_bias, down_bias, layer_scale, mine1, theirs1)
    return merge(keep, swap(give, "ch"))


def solution(mesh):
    in_specs = (
        P(None, ("grp", "lat"), "lon"),
        P("lat", "lon"),
        P("lat", "lon"),
        P(None, None, None, "ch"),
        P(None, "ch"),
        P(None, None, None, "ch"),
        P(None, "ch"),
        P(),
        P(),
        P(None, "lon", "ch"),
        P(),
        P(None, "ch", "lon"),
        P(),
        P(),
    )
    out_specs = P(("grp", "lat"), "lon", "ch")
    return jax.shard_map(body, mesh=mesh, in_specs=in_specs, out_specs=out_specs, check_vma=False)
```
